32 devices in a mesh: dp: 4 (over y, x), fsdp: 4 (over z), crop: 2 (over core).
Axes of the slice: x: 2, y: 2, z: 4, core: 2. Of those that a mesh axis runs over, the one named last changes fastest.
Arguments:
- grad_parts: float32 [8, 848, 1536], P(('dp', 'crop'), None, 'fsdp'), may hold values from -1.5 to 1.5
- student: float32 [848, 1536], P(('dp', 'crop'), 'fsdp'), may hold values from -2 to 2
- teacher: float32 [848, 1536], P(('dp', 'crop'), 'fsdp'), may hold values from -2 to 2
- moment1: float32 [848, 1536], P(('dp', 'crop'), 'fsdp'), may hold values from -0.6 to 0.6
- moment2: float32 [848, 1536], P(('dp', 'crop'), 'fsdp'), may hold values from 0.001 to 0.01
- step_count: int32 [1], replicated, may hold values from 1 to 1999
- pixels: bfloat16 [16, 2, 256, 588], P(('dp', 'fsdp'), 'crop'), may hold values from -5 to 5
- assign: int32 [16, 2], P(('dp', 'fsdp')), may hold values from 0 to 1, each once within a row
Outputs:
- student_new: float32 [848, 1536], P(('dp', 'crop'), 'fsdp')
- moment1_new: float32 [848, 1536], P(('dp', 'crop'), 'fsdp')
- moment2_new: float32 [848, 1536], P(('dp', 'crop'), 'fsdp')
- teacher_new: float32 [848, 1536], P(('dp', 'crop'), 'fsdp')
- student_step: float32 [848, 1536], P(('dp', 'crop'), 'fsdp')
- teacher_tokens: float32 [16, 2, 257, 1536], P(('dp', 'fsdp'))
The draws below stay inside these ranges and needn't reach their ends.
Inputs may be any that keep to these rules, and one draw needn't show every extreme that they name: `assign`: each row holds 0 and 1 once.
All inputs are finite; a program needn't handle non-finite values.
Results may differ from the reference program's by a relative error of at most 0.0003.
Values may be sent and summed in bfloat16 or wider, within the bound.
A program may use at most 64 MiB of HBM per device.

```python
import math
import jax
import jax.numpy as jnp
from jax import lax

D = 1536
GLOBALS = 2
PIX = 588
PATCHES = 256
ROWS = 848
REPLICAS = 8
IMAGES = 16


def table_rows(key):
    base = jax.random.normal(key, (ROWS, D), jnp.float32)
    base = jnp.clip(base, -4.0, 4.0)
    row_index = jnp.arange(ROWS)
    scale = jnp.where(row_index < PIX, 0.05 * PIX ** (-0.5), jnp.where(row_index < PIX + PATCHES, 0.025, jnp.where(row_index == PIX + PATCHES, 0.05, jnp.where(row_index == PIX + PATCHES + 1, 0.01, 0.2))))
    offset = jnp.where(row_index == PIX + PATCHES + 2, 1.0, 0.0)
    return base * scale[:, None] + offset[:, None]


def draw_student(key, part):
    return table_rows(jax.random.fold_in(key, 11))


def draw_teacher(key, part):
    return table_rows(jax.random.fold_in(key, 23))


def raised(entries, stream_key, source, target, shards_of, factor):
    def block_of(axis_at):
        return (jnp.arange(entries.shape[axis_at]) // (entries.shape[axis_at] // shards_of)).reshape((-1,) + (1,) * (entries.ndim - 1 - axis_at))

    first = jax.random.permutation(stream_key, shards_of)[block_of(target)]
    far = (block_of(target) + shards_of // 2) % shards_of
    return jnp.where((block_of(source) == first) | (block_of(source) == far), factor * entries, entries)


def level_of(stream_key, shape, pieces, least, top_value):
    level = 1.0
    for dim, parts in pieces:
        steps = jax.random.uniform(jax.random.fold_in(jax.random.fold_in(stream_key, 6), dim), (parts,), jnp.float32, least / len(pieces), top_value / len(pieces))
        level = level * jnp.repeat(jnp.exp(steps), shape[dim] // parts).reshape((-1,) + (1,) * (len(shape) - 1 - dim))
    return level


def bell_draw(stream_key, dims, deviation, limit, shards=(), kind=jnp.bfloat16):
    result = deviation * jax.random.normal(stream_key, dims, jnp.float32)
    if shards:
        result = result * level_of(stream_key, dims, shards, -0.22, 0.18)
    return jnp.clip(result, -limit, limit).astype(kind)


def bell_draw_with(own_key, dims, scale, limit, shards, heavy, held_as=jnp.bfloat16):
    drawn = scale * jax.random.normal(own_key, dims, jnp.float32)
    if shards:
        drawn = drawn * level_of(own_key, dims, shards, -0.22, 0.18)
    return jnp.clip(raised(drawn, jax.random.fold_in(own_key, 3), *heavy), -limit, limit).astype(held_as)


def setup_inputs(seed: int = 0) -> dict:
    splits = jax.random.split(jax.random.key(seed), 9)
    grad_parts = bell_draw_with(splits[0], (REPLICAS, ROWS, D), 0.25, 1.5, ((0, 8), (2, 4)), (0, 1, 8, 2.0), jnp.float32)
    student = draw_student(jax.random.fold_in(splits[8], 71), 0)
    teacher = draw_teacher(jax.random.fold_in(splits[8], 71), 0)
    moment1 = bell_draw(splits[3], (ROWS, D), 0.1, 0.6, ((0, 8), (1, 4)), jnp.float32)
    moment2 = jnp.clip(jnp.exp(math.log(0.01) - 2.30258502 * jax.random.uniform(splits[4], (ROWS, D), jnp.float32) ** level_of(splits[4], (ROWS, D), ((0, 8), (1, 4)), -0.2, 0.2)), 0.001, 0.01)
    step_count = jax.random.randint(splits[5], (1,), 1, 2000).astype(jnp.int32)
    pixels = bell_draw(splits[6], (IMAGES, GLOBALS, PATCHES, PIX), 1.0, 5.0, ((0, 16), (1, 2)))
    assign = jax.vmap(lambda own: jax.random.permutation(own, 2))(jax.random.split(splits[7], IMAGES)).reshape((IMAGES, GLOBALS)).astype(jnp.int32)
    return {"grad_parts": grad_parts, "student": student, "teacher": teacher, "moment1": moment1, "moment2": moment2, "step_count": step_count, "pixels": pixels, "assign": assign}


beta_one = 0.9
beta_two = 0.999
adam_epsilon = 1e-08
learn_rate = 0.001
weight_decay = 0.04
momentum_base = 0.992
plan_length = 625000.0
norm_epsilon = 1e-06

def optimize(gradient, student, teacher, moment1, moment2, step_count):
    step_value = step_count[0].astype(jnp.float32)
    first_moment = beta_one * moment1 + (1.0 - beta_one) * gradient
    second_moment = beta_two * moment2 + (1.0 - beta_two) * gradient * gradient
    first_fix = 1.0 - jnp.power(jnp.float32(beta_one), step_value)
    second_fix = 1.0 - jnp.power(jnp.float32(beta_two), step_value)
    update = first_moment / first_fix / (jnp.sqrt(second_moment / second_fix) + adam_epsilon) + weight_decay * student
    student_new = student - learn_rate * update
    momentum = 1.0 - (1.0 - momentum_base) * (jnp.cos(math.pi * step_value / plan_length) + 1.0) / 2.0
    teacher_new = momentum * teacher + (1.0 - momentum) * student_new
    return (student_new, first_moment, second_moment, teacher_new, update)

def embed(patches, table):
    count = patches.shape[0]
    pix_size = patches.shape[2]
    patch_count = patches.shape[1]
    width = table.shape[1]
    weight = table[:pix_size]
    position = table[pix_size:pix_size + patch_count]
    extras = table[pix_size + patch_count:]
    flat_patches = patches.reshape(count * patch_count, pix_size).astype(jnp.float32)
    projected = jnp.dot(flat_patches, weight, precision=lax.Precision.HIGHEST, preferred_element_type=jnp.float32)
    projected = projected.reshape(count, patch_count, width) + extras[1] + position
    class_row = jnp.broadcast_to(extras[0], (count, 1, width))
    tokens = jnp.concatenate([class_row, projected], axis=1)
    average = lax.optimization_barrier(jnp.mean(tokens, axis=-1, keepdims=True))
    centered = tokens - average
    variance = lax.optimization_barrier(jnp.mean(centered * centered, axis=-1, keepdims=True))
    return centered * lax.rsqrt(variance + norm_epsilon) * extras[2] + extras[3]

def reference(grad_parts, student, teacher, moment1, moment2, step_count, pixels, assign):
    gradient = lax.optimization_barrier(jnp.sum(grad_parts, axis=0))
    student_new, first_moment, second_moment, teacher_new, update = optimize(gradient, student, teacher, moment1, moment2, step_count)

    def one_image(items):
        crops, order = items
        both = embed(crops, teacher_new)
        return jnp.where((order == 0)[:, None, None], both[0][None], both[1][None])
    teacher_tokens = lax.map(one_image, (pixels, assign))
    return (student_new, first_moment, second_moment, teacher_new, update, teacher_tokens)
```

```python
import functools
import math

import jax
import jax.numpy as jnp
from jax import lax
from jax.experimental import pallas as pl
from jax.experimental.pallas import tpu as pltpu
from jax.sharding import PartitionSpec as P

beta_one = 0.9
beta_two = 0.999
adam_epsilon = 1e-08
learn_rate = 0.001
weight_decay = 0.04
momentum_base = 0.992
plan_length = 625000.0
norm_epsilon = 1e-06


def optimize(gradient, student, teacher, moment1, moment2, step_count):
    step_value = step_count[0].astype(jnp.float32)
    first_moment = beta_one * moment1 + (1.0 - beta_one) * gradient
    second_moment = beta_two * moment2 + (1.0 - beta_two) * gradient * gradient
    first_fix = 1.0 - jnp.power(jnp.float32(beta_one), step_value)
    second_fix = 1.0 - jnp.power(jnp.float32(beta_two), step_value)
    update = (
        first_moment / first_fix / (jnp.sqrt(second_moment / second_fix) + adam_epsilon)
        + weight_decay * student
    )
    student_new = student - learn_rate * update
    momentum = (
        1.0 - (1.0 - momentum_base) * (jnp.cos(math.pi * step_value / plan_length) + 1.0) / 2.0
    )
    teacher_new = momentum * teacher + (1.0 - momentum) * student_new
    return (student_new, first_moment, second_moment, teacher_new, update)


def embed(patches, table):
    count = patches.shape[0]
    pix_size = patches.shape[2]
    patch_count = patches.shape[1]
    width = table.shape[1]
    weight = table[:pix_size]
    position = table[pix_size : pix_size + patch_count]
    extras = table[pix_size + patch_count :]
    flat_patches = patches.reshape(count * patch_count, pix_size).astype(jnp.float32)
    projected = jnp.dot(
        flat_patches, weight, precision=lax.Precision.HIGHEST, preferred_element_type=jnp.float32
    )
    projected = projected.reshape(count, patch_count, width) + extras[1] + position
    class_row = jnp.broadcast_to(extras[0], (count, 1, width))
    tokens = jnp.concatenate([class_row, projected], axis=1)
    average = jnp.mean(tokens, axis=-1, keepdims=True)
    centered = tokens - average
    variance = jnp.mean(centered * centered, axis=-1, keepdims=True)
    return centered * lax.rsqrt(variance + norm_epsilon) * extras[2] + extras[3]


LEVELS = 32767.0
CODES = 256.0
MESH = pl.DeviceIdType.MESH


def padded_rows(rows):
    return -(-(rows + 1) // 16) * 16


def diagonal(count, width):
    first = lax.broadcasted_iota(jnp.int32, (count, width), 0)
    second = lax.broadcasted_iota(jnp.int32, (count, width), 1)
    return first == second


def encode(value, rows):
    count, width = value.shape
    row_index = lax.broadcasted_iota(jnp.int32, (count, width), 0)
    value = jnp.where(row_index < rows, value, 0.0)
    top = jnp.maximum(jnp.max(jnp.abs(value), axis=1, keepdims=True), 1e-30)
    code = jnp.ceil(jnp.log2(top) * CODES + 0.01)
    scaled = value * (jnp.exp2(code * (-1.0 / CODES)) * LEVELS)
    code_row = jnp.sum(
        jnp.where(diagonal(count, width), jnp.broadcast_to(code, (count, width)), 0.0),
        axis=0,
        keepdims=True,
    )
    out = jnp.where(row_index == rows, jnp.broadcast_to(code_row, (count, width)), scaled)
    out = jnp.clip(jnp.round(out), -LEVELS, LEVELS)
    return out.astype(jnp.int32).astype(jnp.int16)


def decode(block, rows):
    count, width = block.shape
    value = block.astype(jnp.int32).astype(jnp.float32)
    code_row = value[rows : rows + 1]
    code = jnp.sum(
        jnp.where(diagonal(count, width), jnp.broadcast_to(code_row, (count, width)), 0.0),
        axis=1,
        keepdims=True,
    )
    return value * (jnp.exp2(code * (1.0 / CODES)) * (1.0 / LEVELS))


def refresh_kernel(
    sizes, grad_ref, pixel_ref, student_ref, teacher_ref, moment1_ref, moment2_ref, fix_ref,
    gradient_ref, table_ref, other_ref,
    out_ref, in_ref, space_ref, out_sem, in_sem, pix_sem, go_sem, come_sem,
):
    DP, F, C = sizes
    rows = student_ref.shape[0]
    d, f, c = lax.axis_index("dp"), lax.axis_index("fsdp"), lax.axis_index("crop")
    me = d * C + c
    N = DP * C

    barrier = pltpu.get_barrier_semaphore()
    for r in range(1, N):
        to = lax.rem(me + r, N)
        pl.semaphore_signal(barrier, inc=1, device_id={"dp": to // C, "crop": lax.rem(to, C)}, device_id_type=MESH)
    for r in range(1, F):
        pl.semaphore_signal(barrier, inc=1, device_id={"fsdp": lax.rem(f + r, F)}, device_id_type=MESH)

    space_ref[...] = jnp.zeros_like(space_ref)
    for j in range(N):
        space_ref[0:rows] = grad_ref[0, j * rows : (j + 1) * rows]
        out_ref[j] = encode(space_ref[...], rows)
    pl.semaphore_wait(barrier, N - 1 + F - 1)

    sends = []
    for r in range(1, N):
        to = lax.rem(me + r, N)
        copy = pltpu.make_async_remote_copy(
            src_ref=out_ref.at[to], dst_ref=in_ref.at[me],
            send_sem=out_sem.at[r], recv_sem=in_sem.at[me],
            device_id={"dp": to // C, "crop": lax.rem(to, C)}, device_id_type=MESH,
        )
        copy.start()
        sends.append(copy)
    pixel_copy = pltpu.make_async_remote_copy(
        src_ref=pixel_ref, dst_ref=other_ref, send_sem=pix_sem.at[0], recv_sem=pix_sem.at[1],
        device_id={"crop": lax.rem(c + 1, C)}, device_id_type=MESH,
    )
    pixel_copy.start()

    total = decode(out_ref[me], rows)
    for r in range(1, N):
        source = lax.rem(me + r, N)
        pltpu.make_async_copy(in_ref.at[source], in_ref.at[source], in_sem.at[source]).wait()
        total = total + decode(in_ref[source], rows)
    gradient = total[0:rows]
    gradient_ref[...] = gradient

    student = student_ref[...]
    first_moment = beta_one * moment1_ref[...] + (1.0 - beta_one) * gradient
    second_moment = beta_two * moment2_ref[...] + (1.0 - beta_two) * gradient * gradient
    update = (
        first_moment / fix_ref[0] / (jnp.sqrt(second_moment / fix_ref[1]) + adam_epsilon)
        + weight_decay * student
    )
    student_new = student - learn_rate * update
    space_ref[0:rows] = fix_ref[2] * teacher_ref[...] + (1.0 - fix_ref[2]) * student_new
    table_ref[f, d, c] = encode(space_ref[...], rows)

    def pass_on(at, to):
        number = len(sends) - (N - 1)
        copy = pltpu.make_async_remote_copy(
            src_ref=table_ref.at[at], dst_ref=table_ref.at[at],
            send_sem=go_sem.at[number], recv_sem=come_sem.at[at],
            device_id=to, device_id_type=MESH,
        )
        copy.start()
        sends.append(copy)

    def arrive(at):
        pltpu.make_async_copy(table_ref.at[at], table_ref.at[at], come_sem.at[at]).wait()

    partner = lax.rem(c + 1, C)
    for q in range(F):
        at = (lax.rem(f + q, F), d, c)
        if q == 0:
            for r in range(1, F):
                pass_on(at, {"fsdp": lax.rem(f + r, F)})
        else:
            arrive(at)
        for r in range(1, DP):
            pass_on(at, {"dp": lax.rem(d + r, DP)})
        pass_on(at, {"crop": partner})
    for q in range(F):
        for r in range(1, DP):
            at = (lax.rem(f + q, F), lax.rem(d + r, DP), c)
            arrive(at)
            pass_on(at, {"crop": partner})
    for q in range(F):
        for r in range(DP):
            arrive((lax.rem(f + q, F), lax.rem(d + r, DP), partner))
    pixel_copy.wait()
    for copy in sends:
        copy.wait_send()


def tokens_kernel(sizes, table_ref, own_ref, other_ref, pick_ref, tokens_ref, flat_ref, high_ref, low_ref, x_ref):
    DP, F, C = sizes
    patch_count, pix_size = own_ref.shape
    columns = table_ref.shape[-1]
    width = flat_ref.shape[1]
    rows = flat_ref.shape[0] // (DP * C)
    base = pix_size + patch_count

    @pl.when(pl.program_id(0) == 0)
    def _():
        for i in range(F):
            for j in range(DP * C):
                block = decode(table_ref[i, j // C, j % C], rows)
                flat_ref[j * rows : (j + 1) * rows, i * columns : (i + 1) * columns] = block[0:rows]
        weight = flat_ref[0:pix_size]
        high = weight.astype(jnp.bfloat16)
        high_ref[...] = high
        low_ref[...] = (weight - high.astype(jnp.float32)).astype(jnp.bfloat16)
        flat_ref[pix_size:base] = flat_ref[pix_size:base] + flat_ref[base + 1 : base + 2]

    gain, shift = flat_ref[base + 2 : base + 3], flat_ref[base + 3 : base + 4]

    def normed(x):
        average = jnp.mean(x, axis=-1, keepdims=True)
        centered = x - average
        variance = jnp.mean(centered * centered, axis=-1, keepdims=True)
        return centered * lax.rsqrt(variance + norm_epsilon) * gain + shift

    pixels = jnp.where(pick_ref[pl.program_id(0)] == 1, own_ref[...], other_ref[...])
    for i in range(F):
        part = slice(i * columns, (i + 1) * columns)
        x_ref[:, part] = (
            jnp.dot(pixels, high_ref[:, part], preferred_element_type=jnp.float32)
            + jnp.dot(pixels, low_ref[:, part], preferred_element_type=jnp.float32)
            + flat_ref[pix_size:base, part]
        )
    tokens_ref[0, 0, 0:1] = normed(flat_ref[base : base + 1])
    tokens_ref[0, 0, 1:] = normed(x_ref[...])


def kernels(grad_parts, student, teacher, moment1, moment2, step_count, pixels, assign, sizes):
    DP, F, C = sizes
    rows, columns = student.shape
    spare = padded_rows(rows)
    step_value = step_count[0].astype(jnp.float32)
    fixes = jnp.stack(
        [
            1.0 - jnp.power(jnp.float32(beta_one), step_value),
            1.0 - jnp.power(jnp.float32(beta_two), step_value),
            1.0 - (1.0 - momentum_base) * (jnp.cos(math.pi * step_value / plan_length) + 1.0) / 2.0,
        ]
    )
    own = pixels[0, 0]
    here = pl.BlockSpec(memory_space=pltpu.VMEM)
    scalars = pl.BlockSpec(memory_space=pltpu.SMEM)
    count = DP * C
    gradient, table, other = pl.pallas_call(
        functools.partial(refresh_kernel, sizes),
        out_shape=(
            jax.ShapeDtypeStruct((rows, columns), jnp.float32),
            jax.ShapeDtypeStruct((F, DP, C, spare, columns), jnp.int16),
            jax.ShapeDtypeStruct(own.shape, own.dtype),
        ),
        in_specs=[here] * 6 + [scalars],
        out_specs=(here,) * 3,
        scratch_shapes=[
            pltpu.VMEM((count, spare, columns), jnp.int16),
            pltpu.VMEM((count, spare, columns), jnp.int16),
            pltpu.VMEM((spare, columns), jnp.float32),
            pltpu.SemaphoreType.DMA((count,)),
            pltpu.SemaphoreType.DMA((count,)),
            pltpu.SemaphoreType.DMA((2,)),
            pltpu.SemaphoreType.DMA((F - 1 + F * DP + F * (DP - 1),)),
            pltpu.SemaphoreType.DMA((F, DP, C)),
        ],
        compiler_params=pltpu.CompilerParams(collective_id=0, has_side_effects=True),
    )(grad_parts, own, student, teacher, moment1, moment2, fixes)
    results = optimize(gradient, student, teacher, moment1, moment2, step_count)
    patch_count, pix_size = own.shape
    width = columns * F
    picks = (assign[0] == lax.axis_index("crop")).astype(jnp.int32)
    tokens = pl.pallas_call(
        functools.partial(tokens_kernel, sizes),
        grid=(C,),
        out_shape=jax.ShapeDtypeStruct((1, C, patch_count + 1, width), jnp.float32),
        in_specs=[here] * 3 + [scalars],
        out_specs=pl.BlockSpec((1, 1, patch_count + 1, width), lambda k: (0, k, 0, 0)),
        scratch_shapes=[
            pltpu.VMEM((rows * count, width), jnp.float32),
            pltpu.VMEM((pix_size, width), jnp.bfloat16),
            pltpu.VMEM((pix_size, width), jnp.bfloat16),
            pltpu.VMEM((patch_count, width), jnp.float32),
        ],
    )(table, own, other, picks)
    return (*results, tokens)


def shards(grad_parts, student, teacher, moment1, moment2, step_count, pixels, assign):
    gradient = lax.psum_scatter(grad_parts[0], ("dp", "crop"), scatter_dimension=0, tiled=True)
    student_new, first_moment, second_moment, teacher_new, update = optimize(
        gradient, student, teacher, moment1, moment2, step_count
    )
    column_block = lax.all_gather(teacher_new, "fsdp", axis=1, tiled=True)
    gathered = lax.all_gather(column_block, ("dp", "crop"), axis=0, tiled=True)
    own_tokens = embed(pixels[:, 0], gathered)
    both = lax.all_gather(own_tokens[:, None], "crop", axis=1, tiled=True)
    teacher_tokens = jnp.where((assign == 0)[:, :, None, None], both[:, 0:1], both[:, 1:2])
    return (student_new, first_moment, second_moment, teacher_new, update, teacher_tokens)


def solution(mesh):
    placed = (
        P(("dp", "crop"), None, "fsdp"),
        P(("dp", "crop"), "fsdp"),
        P(("dp", "crop"), "fsdp"),
        P(("dp", "crop"), "fsdp"),
        P(("dp", "crop"), "fsdp"),
        P(),
        P(("dp", "fsdp"), "crop", None, None),
        P(("dp", "fsdp"), None),
    )
    sizes = (mesh.shape["dp"], mesh.shape["fsdp"], mesh.shape["crop"])

    def run(*args):
        grad_parts, student, pixels = args[0], args[1], args[6]
        fits = (
            student.shape[1] % 128 == 0
            and padded_rows(student.shape[0]) <= student.shape[1]
            and pixels.shape[:2] == (1, 1)
            and grad_parts.shape[0] == 1
            and sizes[2] == 2
        )
        return kernels(*args, sizes) if fits else shards(*args)

    return jax.shard_map(
        run,
        mesh=mesh,
        in_specs=placed,
        out_specs=(
            P(("dp", "crop"), "fsdp"),
            P(("dp", "crop"), "fsdp"),
            P(("dp", "crop"), "fsdp"),
            P(("dp", "crop"), "fsdp"),
            P(("dp", "crop"), "fsdp"),
            P(("dp", "fsdp"), None, None, None),
        ),
        check_vma=False,
    )
```

```python
import functools
import math

import jax
import jax.numpy as jnp
from jax import lax
from jax.experimental import pallas as pl
from jax.experimental.pallas import tpu as pltpu
from jax.sharding import PartitionSpec as P

beta_one = 0.9
beta_two = 0.999
adam_epsilon = 1e-08
learn_rate = 0.001
weight_decay = 0.04
momentum_base = 0.992
plan_length = 625000.0
norm_epsilon = 1e-06


def optimize(gradient, student, teacher, moment1, moment2, step_count):
    step_value = step_count[0].astype(jnp.float32)
    first_moment = beta_one * moment1 + (1.0 - beta_one) * gradient
    second_moment = beta_two * moment2 + (1.0 - beta_two) * gradient * gradient
    first_fix = 1.0 - jnp.power(jnp.float32(beta_one), step_value)
    second_fix = 1.0 - jnp.power(jnp.float32(beta_two), step_value)
    update = (
        first_moment / first_fix / (jnp.sqrt(second_moment / second_fix) + adam_epsilon)
        + weight_decay * student
    )
    student_new = student - learn_rate * update
    momentum = (
        1.0 - (1.0 - momentum_base) * (jnp.cos(math.pi * step_value / plan_length) + 1.0) / 2.0
    )
    teacher_new = momentum * teacher + (1.0 - momentum) * student_new
    return (student_new, first_moment, second_moment, teacher_new, update)


def embed(patches, table):
    count = patches.shape[0]
    pix_size = patches.shape[2]
    patch_count = patches.shape[1]
    width = table.shape[1]
    weight = table[:pix_size]
    position = table[pix_size : pix_size + patch_count]
    extras = table[pix_size + patch_count :]
    flat_patches = patches.reshape(count * patch_count, pix_size).astype(jnp.float32)
    projected = jnp.dot(
        flat_patches, weight, precision=lax.Precision.HIGHEST, preferred_element_type=jnp.float32
    )
    projected = projected.reshape(count, patch_count, width) + extras[1] + position
    class_row = jnp.broadcast_to(extras[0], (count, 1, width))
    tokens = jnp.concatenate([class_row, projected], axis=1)
    average = jnp.mean(tokens, axis=-1, keepdims=True)
    centered = tokens - average
    variance = jnp.mean(centered * centered, axis=-1, keepdims=True)
    return centered * lax.rsqrt(variance + norm_epsilon) * extras[2] + extras[3]


LEVELS = 32767.0
CODES = 256.0
MESH = pl.DeviceIdType.MESH


def padded_rows(rows):
    return -(-(rows + 1) // 16) * 16


def diagonal(count, width):
    first = lax.broadcasted_iota(jnp.int32, (count, width), 0)
    second = lax.broadcasted_iota(jnp.int32, (count, width), 1)
    return first == second


def encode(value, rows):
    count, width = value.shape
    row_index = lax.broadcasted_iota(jnp.int32, (count, width), 0)
    value = jnp.where(row_index < rows, value, 0.0)
    top = jnp.maximum(jnp.max(jnp.abs(value), axis=1, keepdims=True), 1e-30)
    code = jnp.ceil(jnp.log2(top) * CODES + 0.01)
    scaled = value * (jnp.exp2(code * (-1.0 / CODES)) * LEVELS)
    code_row = jnp.sum(
        jnp.where(diagonal(count, width), jnp.broadcast_to(code, (count, width)), 0.0),
        axis=0,
        keepdims=True,
    )
    out = jnp.where(row_index == rows, jnp.broadcast_to(code_row, (count, width)), scaled)
    out = jnp.clip(jnp.round(out), -LEVELS, LEVELS)
    return out.astype(jnp.int32).astype(jnp.int16)


def decode(block, rows):
    count, width = block.shape
    value = block.astype(jnp.int32).astype(jnp.float32)
    code_row = value[rows : rows + 1]
    code = jnp.sum(
        jnp.where(diagonal(count, width), jnp.broadcast_to(code_row, (count, width)), 0.0),
        axis=1,
        keepdims=True,
    )
    return value * (jnp.exp2(code * (1.0 / CODES)) * (1.0 / LEVELS))


def refresh_kernel(
    sizes, grad_ref, pixel_ref, student_ref, teacher_ref, moment1_ref, moment2_ref, fix_ref,
    gradient_ref, table_ref, other_ref,
    out_ref, in_ref, space_ref, out_sem, in_sem, pix_sem, go_sem, come_sem,
):
    DP, F, C = sizes
    rows = student_ref.shape[0]
    d, f, c = lax.axis_index("dp"), lax.axis_index("fsdp"), lax.axis_index("crop")
    me = d * C + c
    N = DP * C

    barrier = pltpu.get_barrier_semaphore()
    for r in range(1, N):
        to = lax.rem(me + r, N)
        pl.semaphore_signal(barrier, inc=1, device_id={"dp": to // C, "crop": lax.rem(to, C)}, device_id_type=MESH)
    for r in range(1, F):
        pl.semaphore_signal(barrier, inc=1, device_id={"fsdp": lax.rem(f + r, F)}, device_id_type=MESH)

    space_ref[...] = jnp.zeros_like(space_ref)
    blocks = []
    for j in range(N):
        space_ref[0:rows] = grad_ref[0, j * rows : (j + 1) * rows]
        out_ref[j] = encode(space_ref[...], rows)
        if j == 0:
            pl.semaphore_wait(barrier, N - 1 + F - 1)
        copy = pltpu.make_async_remote_copy(
            src_ref=out_ref.at[j], dst_ref=in_ref.at[me],
            send_sem=out_sem.at[j], recv_sem=in_sem.at[me],
            device_id={"dp": j // C, "crop": j % C}, device_id_type=MESH,
        )
        pl.when(j != me)(copy.start)
        blocks.append(copy)
    sends = []
    pixel_copy = pltpu.make_async_remote_copy(
        src_ref=pixel_ref, dst_ref=other_ref, send_sem=pix_sem.at[0], recv_sem=pix_sem.at[1],
        device_id={"crop": lax.rem(c + 1, C)}, device_id_type=MESH,
    )
    pixel_copy.start()

    total = decode(out_ref[me], rows)
    for r in range(1, N):
        source = lax.rem(me + r, N)
        pltpu.make_async_copy(in_ref.at[source], in_ref.at[source], in_sem.at[source]).wait()
        total = total + decode(in_ref[source], rows)
    gradient = total[0:rows]
    gradient_ref[...] = gradient

    student = student_ref[...]
    first_moment = beta_one * moment1_ref[...] + (1.0 - beta_one) * gradient
    second_moment = beta_two * moment2_ref[...] + (1.0 - beta_two) * gradient * gradient
    update = (
        first_moment / fix_ref[0] / (jnp.sqrt(second_moment / fix_ref[1]) + adam_epsilon)
        + weight_decay * student
    )
    student_new = student - learn_rate * update
    space_ref[0:rows] = fix_ref[2] * teacher_ref[...] + (1.0 - fix_ref[2]) * student_new
    table_ref[f, d, c] = encode(space_ref[...], rows)

    def pass_on(at, to):
        number = len(sends)
        copy = pltpu.make_async_remote_copy(
            src_ref=table_ref.at[at], dst_ref=table_ref.at[at],
            send_sem=go_sem.at[number], recv_sem=come_sem.at[at],
            device_id=to, device_id_type=MESH,
        )
        copy.start()
        sends.append(copy)

    def arrive(at):
        pltpu.make_async_copy(table_ref.at[at], table_ref.at[at], come_sem.at[at]).wait()

    partner = lax.rem(c + 1, C)
    row, column = d // 2, lax.rem(d, 2)
    beside = row * 2 + 1 - column
    across = (1 - row) * 2 + column
    corner = (1 - row) * 2 + 1 - column
    for q in range(F):
        at = (lax.rem(f + q, F), d, c)
        if q == 0:
            for r in range(1, F):
                pass_on(at, {"fsdp": lax.rem(f + r, F)})
        else:
            arrive(at)
        pass_on(at, {"dp": beside})
        pass_on(at, {"dp": across})
        pass_on(at, {"crop": partner})
    for q in range(F):
        for near, far in ((beside, across), (across, beside)):
            at = (lax.rem(f + q, F), near, c)
            arrive(at)
            if (q % 2 == 0) == (near is beside):
                pass_on(at, {"dp": far})
            pass_on(at, {"crop": partner})
    for q in range(F):
        at = (lax.rem(f + q, F), corner, c)
        arrive(at)
        pass_on(at, {"crop": partner})
    for q in range(F):
        for r in range(DP):
            arrive((lax.rem(f + q, F), lax.rem(d + r, DP), partner))
    pixel_copy.wait()
    for j, copy in enumerate(blocks):
        pl.when(j != me)(copy.wait_send)
    for copy in sends:
        copy.wait_send()


def tokens_kernel(sizes, table_ref, own_ref, other_ref, pick_ref, tokens_ref, flat_ref, high_ref, low_ref, x_ref):
    DP, F, C = sizes
    pix_size, patch_count = own_ref.shape
    columns = table_ref.shape[-1]
    width = flat_ref.shape[1]
    rows = flat_ref.shape[0] // (DP * C)
    base = pix_size + patch_count
    over = (((0,), (0,)), ((), ()))

    for i in range(F):
        for j in range(DP * C):
            block = decode(table_ref[i, j // C, j % C], rows)
            flat_ref[j * rows : (j + 1) * rows, i * columns : (i + 1) * columns] = block[0:rows]
    weight = flat_ref[0:pix_size]
    high = weight.astype(jnp.bfloat16)
    high_ref[...] = high
    low_ref[...] = (weight - high.astype(jnp.float32)).astype(jnp.bfloat16)
    flat_ref[pix_size:base] = flat_ref[pix_size:base] + flat_ref[base + 1 : base + 2]

    gain, shift = flat_ref[base + 2 : base + 3], flat_ref[base + 3 : base + 4]

    def normed(x):
        average = jnp.mean(x, axis=-1, keepdims=True)
        centered = x - average
        variance = jnp.mean(centered * centered, axis=-1, keepdims=True)
        return centered * lax.rsqrt(variance + norm_epsilon) * gain + shift

    class_row = normed(flat_ref[base : base + 1])
    for k in range(C):
        pixels = jnp.where(pick_ref[0, k] == lax.axis_index("crop"), own_ref[...], other_ref[...])
        for i in range(F):
            part = slice(i * columns, (i + 1) * columns)
            x_ref[:, part] = (
                lax.dot_general(pixels, high_ref[:, part], over, preferred_element_type=jnp.float32)
                + lax.dot_general(pixels, low_ref[:, part], over, preferred_element_type=jnp.float32)
                + flat_ref[pix_size:base, part]
            )
        tokens_ref[0:1, k] = class_row
        step = 32
        for start in range(0, patch_count, step):
            rows_now = normed(x_ref[start : start + step])
            tokens_ref[start + 1 : start + 1 + step, k] = rows_now


def kernels(grad_parts, student, teacher, moment1, moment2, step_count, pixels, assign, sizes):
    DP, F, C = sizes
    rows, columns = student.shape
    spare = padded_rows(rows)
    step_value = step_count[0].astype(jnp.float32)
    fixes = jnp.stack(
        [
            1.0 - jnp.power(jnp.float32(beta_one), step_value),
            1.0 - jnp.power(jnp.float32(beta_two), step_value),
            1.0 - (1.0 - momentum_base) * (jnp.cos(math.pi * step_value / plan_length) + 1.0) / 2.0,
        ]
    )
    own = pixels[0, 0].T
    here = pl.BlockSpec(memory_space=pltpu.VMEM)
    scalars = pl.BlockSpec(memory_space=pltpu.SMEM)
    count = DP * C
    gradient, table, other = pl.pallas_call(
        functools.partial(refresh_kernel, sizes),
        out_shape=(
            jax.ShapeDtypeStruct((rows, columns), jnp.float32),
            jax.ShapeDtypeStruct((F, DP, C, spare, columns), jnp.int16),
            jax.ShapeDtypeStruct(own.shape, own.dtype),
        ),
        in_specs=[here] * 6 + [scalars],
        out_specs=(here,) * 3,
        scratch_shapes=[
            pltpu.VMEM((count, spare, columns), jnp.int16),
            pltpu.VMEM((count, spare, columns), jnp.int16),
            pltpu.VMEM((spare, columns), jnp.float32),
            pltpu.SemaphoreType.DMA((count,)),
            pltpu.SemaphoreType.DMA((count,)),
            pltpu.SemaphoreType.DMA((2,)),
            pltpu.SemaphoreType.DMA((F - 1 + F * 7,)),
            pltpu.SemaphoreType.DMA((F, DP, C)),
        ],
        compiler_params=pltpu.CompilerParams(collective_id=0, has_side_effects=True),
    )(grad_parts, own, student, teacher, moment1, moment2, fixes)
    results = optimize(gradient, student, teacher, moment1, moment2, step_count)
    pix_size, patch_count = own.shape
    width = columns * F
    tokens = pl.pallas_call(
        functools.partial(tokens_kernel, sizes),
        out_shape=jax.ShapeDtypeStruct((patch_count + 1, C, width), jnp.float32),
        in_specs=[here] * 3 + [scalars],
        out_specs=here,
        scratch_shapes=[
            pltpu.VMEM((rows * count, width), jnp.float32),
            pltpu.VMEM((pix_size, width), jnp.bfloat16),
            pltpu.VMEM((pix_size, width), jnp.bfloat16),
            pltpu.VMEM((patch_count, width), jnp.float32),
        ],
    )(table, own, other, assign)
    return (*results, tokens.transpose(1, 0, 2)[None])


def shards(grad_parts, student, teacher, moment1, moment2, step_count, pixels, assign):
    gradient = lax.psum_scatter(grad_parts[0], ("dp", "crop"), scatter_dimension=0, tiled=True)
    student_new, first_moment, second_moment, teacher_new, update = optimize(
        gradient, student, teacher, moment1, moment2, step_count
    )
    column_block = lax.all_gather(teacher_new, "fsdp", axis=1, tiled=True)
    gathered = lax.all_gather(column_block, ("dp", "crop"), axis=0, tiled=True)
    own_tokens = embed(pixels[:, 0], gathered)
    both = lax.all_gather(own_tokens[:, None], "crop", axis=1, tiled=True)
    teacher_tokens = jnp.where((assign == 0)[:, :, None, None], both[:, 0:1], both[:, 1:2])
    return (student_new, first_moment, second_moment, teacher_new, update, teacher_tokens)


def solution(mesh):
    placed = (
        P(("dp", "crop"), None, "fsdp"),
        P(("dp", "crop"), "fsdp"),
        P(("dp", "crop"), "fsdp"),
        P(("dp", "crop"), "fsdp"),
        P(("dp", "crop"), "fsdp"),
        P(),
        P(("dp", "fsdp"), "crop", None, None),
        P(("dp", "fsdp"), None),
    )
    sizes = (mesh.shape["dp"], mesh.shape["fsdp"], mesh.shape["crop"])

    def run(*args):
        grad_parts, student, pixels = args[0], args[1], args[6]
        fits = (
            student.shape[1] % 128 == 0
            and padded_rows(student.shape[0]) <= student.shape[1]
            and pixels.shape[:2] == (1, 1)
            and grad_parts.shape[0] == 1
            and sizes[0] == 4
            and sizes[2] == 2
        )
        return kernels(*args, sizes) if fits else shards(*args)

    return jax.shard_map(
        run,
        mesh=mesh,
        in_specs=placed,
        out_specs=(
            P(("dp", "crop"), "fsdp"),
            P(("dp", "crop"), "fsdp"),
            P(("dp", "crop"), "fsdp"),
            P(("dp", "crop"), "fsdp"),
            P(("dp", "crop"), "fsdp"),
            P(("dp", "fsdp"), None, None, None),
        ),
        check_vma=False,
    )
```

```python
import functools
import math

import jax
import jax.numpy as jnp
from jax import lax
from jax.experimental import pallas as pl
from jax.experimental.pallas import tpu as pltpu
from jax.sharding import PartitionSpec as P

beta_one = 0.9
beta_two = 0.999
adam_epsilon = 1e-08
learn_rate = 0.001
weight_decay = 0.04
momentum_base = 0.992
plan_length = 625000.0
norm_epsilon = 1e-06


def optimize(gradient, student, teacher, moment1, moment2, step_count):
    step_value = step_count[0].astype(jnp.float32)
    first_moment = beta_one * moment1 + (1.0 - beta_one) * gradient
    second_moment = beta_two * moment2 + (1.0 - beta_two) * gradient * gradient
    first_fix = 1.0 - jnp.power(jnp.float32(beta_one), step_value)
    second_fix = 1.0 - jnp.power(jnp.float32(beta_two), step_value)
    update = (
        first_moment / first_fix / (jnp.sqrt(second_moment / second_fix) + adam_epsilon)
        + weight_decay * student
    )
    student_new = student - learn_rate * update
    momentum = (
        1.0 - (1.0 - momentum_base) * (jnp.cos(math.pi * step_value / plan_length) + 1.0) / 2.0
    )
    teacher_new = momentum * teacher + (1.0 - momentum) * student_new
    return (student_new, first_moment, second_moment, teacher_new, update)


def embed(patches, table):
    count = patches.shape[0]
    pix_size = patches.shape[2]
    patch_count = patches.shape[1]
    width = table.shape[1]
    weight = table[:pix_size]
    position = table[pix_size : pix_size + patch_count]
    extras = table[pix_size + patch_count :]
    flat_patches = patches.reshape(count * patch_count, pix_size).astype(jnp.float32)
    projected = jnp.dot(
        flat_patches, weight, precision=lax.Precision.HIGHEST, preferred_element_type=jnp.float32
    )
    projected = projected.reshape(count, patch_count, width) + extras[1] + position
    class_row = jnp.broadcast_to(extras[0], (count, 1, width))
    tokens = jnp.concatenate([class_row, projected], axis=1)
    average = jnp.mean(tokens, axis=-1, keepdims=True)
    centered = tokens - average
    variance = jnp.mean(centered * centered, axis=-1, keepdims=True)
    return centered * lax.rsqrt(variance + norm_epsilon) * extras[2] + extras[3]


LEVELS = 32767.0
CODES = 256.0
MESH = pl.DeviceIdType.MESH


def padded_rows(rows):
    return -(-(rows + 1) // 16) * 16


def lanes_of(count):
    return -(-count // 128) * 128


def diagonal(count, width):
    first = lax.broadcasted_iota(jnp.int32, (count, width), 0)
    second = lax.broadcasted_iota(jnp.int32, (count, width), 1)
    return first == second


def encode(value, rows):
    count, width = value.shape
    row_index = lax.broadcasted_iota(jnp.int32, (count, width), 0)
    value = jnp.where(row_index < rows, value, 0.0)
    top = jnp.maximum(jnp.max(jnp.abs(value), axis=1, keepdims=True), 1e-30)
    code = jnp.ceil(jnp.log2(top) * CODES + 0.01)
    scaled = value * (jnp.exp2(code * (-1.0 / CODES)) * LEVELS)
    near = jnp.where(diagonal(count, lanes_of(count)), code, 0.0)
    code_row = jnp.sum(near, axis=0, keepdims=True)
    if width > lanes_of(count):
        rest = jnp.zeros((1, width - lanes_of(count)), jnp.float32)
        code_row = jnp.concatenate([code_row, rest], axis=1)
    out = jnp.where(row_index == rows, jnp.broadcast_to(code_row, (count, width)), scaled)
    out = jnp.clip(jnp.round(out), -LEVELS, LEVELS)
    return out.astype(jnp.int32).astype(jnp.int16)


def decode(block, rows):
    count, width = block.shape
    value = block.astype(jnp.int32).astype(jnp.float32)
    code_row = value[rows : rows + 1, : lanes_of(count)]
    near = jnp.where(diagonal(count, lanes_of(count)), code_row, 0.0)
    code = jnp.sum(near, axis=1, keepdims=True)
    return value * (jnp.exp2(code * (1.0 / CODES)) * (1.0 / LEVELS))


def refresh_kernel(
    sizes, grad_ref, pixel_ref, student_ref, teacher_ref, moment1_ref, moment2_ref, fix_ref,
    gradient_ref, table_ref, other_ref,
    all_ref, pre_ref, out_ref, in_ref, space_ref, pair_sem, out_sem, in_sem, pix_sem, go_sem, come_sem,
):
    DP, F, C = sizes
    rows = student_ref.shape[0]
    d, f, c = lax.axis_index("dp"), lax.axis_index("fsdp"), lax.axis_index("crop")
    partner = lax.rem(c + 1, C)

    barrier = pltpu.get_barrier_semaphore()
    pl.semaphore_signal(barrier, inc=1, device_id={"crop": partner}, device_id_type=MESH)
    for r in range(1, DP):
        pl.semaphore_signal(barrier, inc=1, device_id={"dp": lax.rem(d + r, DP)}, device_id_type=MESH)
    for r in range(1, F):
        pl.semaphore_signal(barrier, inc=1, device_id={"fsdp": lax.rem(f + r, F)}, device_id_type=MESH)

    for b in range(DP):
        for k in range(C):
            j = b * C + k
            all_ref[k, b, 0:rows] = grad_ref[0, j * rows : (j + 1) * rows]
            all_ref[k, b, rows:] = jnp.zeros((all_ref.shape[2] - rows, all_ref.shape[3]), jnp.float32)
    pl.semaphore_wait(barrier, DP - 1 + 1 + F - 1)
    order = [DP - r for r in range(1, DP)] + [0]
    sends = []
    for r in order:
        at = lax.rem(d + r, DP)
        copy = pltpu.make_async_remote_copy(
            src_ref=all_ref.at[partner, at], dst_ref=pre_ref.at[lax.rem(d + r, DP)],
            send_sem=pair_sem.at[0, r], recv_sem=pair_sem.at[1, r],
            device_id={"crop": partner}, device_id_type=MESH,
        )
        copy.start()
        sends.append(copy)
    blocks = []
    total = None
    for number, r in enumerate(order):
        at = lax.rem(d + r, DP)
        sends[number].wait_recv()
        chip = all_ref[c, at] + pre_ref[at]
        if r == 0:
            total = chip
            break
        out_ref[r] = encode(chip, rows)
        copy = pltpu.make_async_remote_copy(
            src_ref=out_ref.at[r], dst_ref=in_ref.at[r],
            send_sem=out_sem.at[r], recv_sem=in_sem.at[r],
            device_id={"dp": at}, device_id_type=MESH,
        )
        copy.start()
        blocks.append(copy)
    pixel_copy = pltpu.make_async_remote_copy(
        src_ref=pixel_ref, dst_ref=other_ref, send_sem=pix_sem.at[0], recv_sem=pix_sem.at[1],
        device_id={"crop": lax.rem(c + 1, C)}, device_id_type=MESH,
    )
    pixel_copy.start()

    for number, copy in enumerate(blocks):
        copy.wait_recv()
        total = total + decode(in_ref[order[number]], rows)
    gradient = total[0:rows]
    gradient_ref[...] = gradient

    student = student_ref[...]
    first_moment = beta_one * moment1_ref[...] + (1.0 - beta_one) * gradient
    second_moment = beta_two * moment2_ref[...] + (1.0 - beta_two) * gradient * gradient
    update = (
        first_moment / fix_ref[0] / (jnp.sqrt(second_moment / fix_ref[1]) + adam_epsilon)
        + weight_decay * student
    )
    student_new = student - learn_rate * update
    space_ref[rows:] = jnp.zeros((space_ref.shape[0] - rows, space_ref.shape[1]), jnp.float32)
    space_ref[0:rows] = fix_ref[2] * teacher_ref[...] + (1.0 - fix_ref[2]) * student_new
    table_ref[f, d, c] = encode(space_ref[...], rows)

    def pass_on(at, to):
        number = len(sends) - DP
        copy = pltpu.make_async_remote_copy(
            src_ref=table_ref.at[at], dst_ref=table_ref.at[at],
            send_sem=go_sem.at[number], recv_sem=come_sem.at[at],
            device_id=to, device_id_type=MESH,
        )
        copy.start()
        sends.append(copy)

    def arrive(at):
        pltpu.make_async_copy(table_ref.at[at], table_ref.at[at], come_sem.at[at]).wait()

    row, column = d // 2, lax.rem(d, 2)
    beside = row * 2 + 1 - column
    across = (1 - row) * 2 + column
    corner = (1 - row) * 2 + 1 - column
    for q in range(F):
        at = (lax.rem(f + q, F), d, c)
        if q == 0:
            for r in range(1, F):
                pass_on(at, {"fsdp": lax.rem(f + r, F)})
        else:
            arrive(at)
        pass_on(at, {"dp": beside})
        pass_on(at, {"dp": across})
        pass_on(at, {"crop": partner})
    for q in range(F):
        for near, far in ((beside, across), (across, beside)):
            at = (lax.rem(f + q, F), near, c)
            arrive(at)
            if (q % 2 == 0) == (near is beside):
                pass_on(at, {"dp": far})
            pass_on(at, {"crop": partner})
    for q in range(F):
        at = (lax.rem(f + q, F), corner, c)
        arrive(at)
        pass_on(at, {"crop": partner})
    for q in range(F):
        for r in range(DP):
            arrive((lax.rem(f + q, F), lax.rem(d + r, DP), partner))
    pixel_copy.wait()
    for copy in blocks + sends:
        copy.wait_send()


def tokens_kernel(
    sizes, table_ref, own_ref, other_ref, gradient_ref, student_ref, teacher_ref, moment1_ref, moment2_ref,
    pick_ref, fix_ref,
    student_out, moment1_out, moment2_out, teacher_out, update_out, tokens_ref,
    flat_ref, high_ref, low_ref, x_ref,
):
    DP, F, C = sizes
    student, gradient = student_ref[...], gradient_ref[...]
    first_moment = beta_one * moment1_ref[...] + (1.0 - beta_one) * gradient
    second_moment = beta_two * moment2_ref[...] + (1.0 - beta_two) * gradient * gradient
    update = (
        first_moment / fix_ref[0] / (jnp.sqrt(second_moment / fix_ref[1]) + adam_epsilon)
        + weight_decay * student
    )
    student_new = student - learn_rate * update
    student_out[...] = student_new
    moment1_out[...] = first_moment
    moment2_out[...] = second_moment
    teacher_out[...] = fix_ref[2] * teacher_ref[...] + (1.0 - fix_ref[2]) * student_new
    update_out[...] = update
    pix_size, patch_count = own_ref.shape
    columns = table_ref.shape[-1]
    width = flat_ref.shape[1]
    rows = flat_ref.shape[0] // (DP * C)
    base = pix_size + patch_count
    over = (((0,), (0,)), ((), ()))

    for i in range(F):
        for j in range(DP * C):
            block = decode(table_ref[i, j // C, j % C], rows)
            flat_ref[j * rows : (j + 1) * rows, i * columns : (i + 1) * columns] = block[0:rows]
    weight = flat_ref[0:pix_size]
    high = weight.astype(jnp.bfloat16)
    high_ref[...] = high
    low_ref[...] = (weight - high.astype(jnp.float32)).astype(jnp.bfloat16)
    flat_ref[pix_size:base] = flat_ref[pix_size:base] + flat_ref[base + 1 : base + 2]

    gain, shift = flat_ref[base + 2 : base + 3], flat_ref[base + 3 : base + 4]

    def normed(x):
        average = jnp.mean(x, axis=-1, keepdims=True)
        centered = x - average
        variance = jnp.mean(centered * centered, axis=-1, keepdims=True)
        return centered * lax.rsqrt(variance + norm_epsilon) * gain + shift

    class_row = normed(flat_ref[base : base + 1])
    for k in range(C):
        pixels = jnp.where(pick_ref[0, k] == lax.axis_index("crop"), own_ref[...], other_ref[...])
        for i in range(F):
            part = slice(i * columns, (i + 1) * columns)
            x_ref[:, part] = (
                lax.dot_general(pixels, high_ref[:, part], over, preferred_element_type=jnp.float32)
                + lax.dot_general(pixels, low_ref[:, part], over, preferred_element_type=jnp.float32)
                + flat_ref[pix_size:base, part]
            )
        tokens_ref[0:1, k] = class_row
        step = 32
        for start in range(0, patch_count, step):
            rows_now = normed(x_ref[start : start + step])
            tokens_ref[start + 1 : start + 1 + step, k] = rows_now


def kernels(grad_parts, student, teacher, moment1, moment2, step_count, pixels, assign, sizes):
    DP, F, C = sizes
    rows, columns = student.shape
    spare = padded_rows(rows)
    step_value = step_count[0].astype(jnp.float32)
    fixes = jnp.stack(
        [
            1.0 - jnp.power(jnp.float32(beta_one), step_value),
            1.0 - jnp.power(jnp.float32(beta_two), step_value),
            1.0 - (1.0 - momentum_base) * (jnp.cos(math.pi * step_value / plan_length) + 1.0) / 2.0,
        ]
    )
    own = pixels[0, 0].T
    here = pl.BlockSpec(memory_space=pltpu.VMEM)
    scalars = pl.BlockSpec(memory_space=pltpu.SMEM)
    count = DP * C
    gradient, table, other = pl.pallas_call(
        functools.partial(refresh_kernel, sizes),
        out_shape=(
            jax.ShapeDtypeStruct((rows, columns), jnp.float32),
            jax.ShapeDtypeStruct((F, DP, C, spare, columns), jnp.int16),
            jax.ShapeDtypeStruct(own.shape, own.dtype),
        ),
        in_specs=[here] * 6 + [scalars],
        out_specs=(here,) * 3,
        scratch_shapes=[
            pltpu.VMEM((C, DP, spare, columns), jnp.float32),
            pltpu.VMEM((DP, spare, columns), jnp.float32),
            pltpu.VMEM((DP, spare, columns), jnp.int16),
            pltpu.VMEM((DP, spare, columns), jnp.int16),
            pltpu.VMEM((spare, columns), jnp.float32),
            pltpu.SemaphoreType.DMA((2, DP)),
            pltpu.SemaphoreType.DMA((DP,)),
            pltpu.SemaphoreType.DMA((DP,)),
            pltpu.SemaphoreType.DMA((2,)),
            pltpu.SemaphoreType.DMA((F - 1 + F * 7,)),
            pltpu.SemaphoreType.DMA((F, DP, C)),
        ],
        compiler_params=pltpu.CompilerParams(collective_id=0, has_side_effects=True),
    )(grad_parts, own, student, teacher, moment1, moment2, fixes)
    pix_size, patch_count = own.shape
    width = columns * F
    *results, tokens = pl.pallas_call(
        functools.partial(tokens_kernel, sizes),
        out_shape=(jax.ShapeDtypeStruct((rows, columns), jnp.float32),) * 5
        + (jax.ShapeDtypeStruct((patch_count + 1, C, width), jnp.float32),),
        in_specs=[here] * 8 + [scalars] * 2,
        out_specs=(here,) * 6,
        scratch_shapes=[
            pltpu.VMEM((rows * count, width), jnp.float32),
            pltpu.VMEM((pix_size, width), jnp.bfloat16),
            pltpu.VMEM((pix_size, width), jnp.bfloat16),
            pltpu.VMEM((patch_count, width), jnp.float32),
        ],
    )(table, own, other, gradient, student, teacher, moment1, moment2, assign, fixes)
    return (*results, tokens.transpose(1, 0, 2)[None])


def shards(grad_parts, student, teacher, moment1, moment2, step_count, pixels, assign):
    gradient = lax.psum_scatter(grad_parts[0], ("dp", "crop"), scatter_dimension=0, tiled=True)
    student_new, first_moment, second_moment, teacher_new, update = optimize(
        gradient, student, teacher, moment1, moment2, step_count
    )
    column_block = lax.all_gather(teacher_new, "fsdp", axis=1, tiled=True)
    gathered = lax.all_gather(column_block, ("dp", "crop"), axis=0, tiled=True)
    own_tokens = embed(pixels[:, 0], gathered)
    both = lax.all_gather(own_tokens[:, None], "crop", axis=1, tiled=True)
    teacher_tokens = jnp.where((assign == 0)[:, :, None, None], both[:, 0:1], both[:, 1:2])
    return (student_new, first_moment, second_moment, teacher_new, update, teacher_tokens)


def solution(mesh):
    placed = (
        P(("dp", "crop"), None, "fsdp"),
        P(("dp", "crop"), "fsdp"),
        P(("dp", "crop"), "fsdp"),
        P(("dp", "crop"), "fsdp"),
        P(("dp", "crop"), "fsdp"),
        P(),
        P(("dp", "fsdp"), "crop", None, None),
        P(("dp", "fsdp"), None),
    )
    sizes = (mesh.shape["dp"], mesh.shape["fsdp"], mesh.shape["crop"])

    def run(*args):
        grad_parts, student, pixels = args[0], args[1], args[6]
        fits = (
            student.shape[1] % 128 == 0
            and padded_rows(student.shape[0]) <= student.shape[1]
            and pixels.shape[:2] == (1, 1)
            and grad_parts.shape[0] == 1
            and sizes[0] == 4
            and sizes[2] == 2
        )
        return kernels(*args, sizes) if fits else shards(*args)

    return jax.shard_map(
        run,
        mesh=mesh,
        in_specs=placed,
        out_specs=(
            P(("dp", "crop"), "fsdp"),
            P(("dp", "crop"), "fsdp"),
            P(("dp", "crop"), "fsdp"),
            P(("dp", "crop"), "fsdp"),
            P(("dp", "crop"), "fsdp"),
            P(("dp", "fsdp"), None, None, None),
        ),
        check_vma=False,
    )
```

```python
import functools
import math

import jax
import jax.numpy as jnp
from jax import lax
from jax.experimental import pallas as pl
from jax.experimental.pallas import tpu as pltpu
from jax.sharding import PartitionSpec as P

beta_one = 0.9
beta_two = 0.999
adam_epsilon = 1e-08
learn_rate = 0.001
weight_decay = 0.04
momentum_base = 0.992
plan_length = 625000.0
norm_epsilon = 1e-06


def optimize(gradient, student, teacher, moment1, moment2, step_count):
    step_value = step_count[0].astype(jnp.float32)
    first_moment = beta_one * moment1 + (1.0 - beta_one) * gradient
    second_moment = beta_two * moment2 + (1.0 - beta_two) * gradient * gradient
    first_fix = 1.0 - jnp.power(jnp.float32(beta_one), step_value)
    second_fix = 1.0 - jnp.power(jnp.float32(beta_two), step_value)
    update = (
        first_moment / first_fix / (jnp.sqrt(second_moment / second_fix) + adam_epsilon)
        + weight_decay * student
    )
    student_new = student - learn_rate * update
    momentum = (
        1.0 - (1.0 - momentum_base) * (jnp.cos(math.pi * step_value / plan_length) + 1.0) / 2.0
    )
    teacher_new = momentum * teacher + (1.0 - momentum) * student_new
    return (student_new, first_moment, second_moment, teacher_new, update)


def embed(patches, table):
    count = patches.shape[0]
    pix_size = patches.shape[2]
    patch_count = patches.shape[1]
    width = table.shape[1]
    weight = table[:pix_size]
    position = table[pix_size : pix_size + patch_count]
    extras = table[pix_size + patch_count :]
    flat_patches = patches.reshape(count * patch_count, pix_size).astype(jnp.float32)
    projected = jnp.dot(
        flat_patches, weight, precision=lax.Precision.HIGHEST, preferred_element_type=jnp.float32
    )
    projected = projected.reshape(count, patch_count, width) + extras[1] + position
    class_row = jnp.broadcast_to(extras[0], (count, 1, width))
    tokens = jnp.concatenate([class_row, projected], axis=1)
    average = jnp.mean(tokens, axis=-1, keepdims=True)
    centered = tokens - average
    variance = jnp.mean(centered * centered, axis=-1, keepdims=True)
    return centered * lax.rsqrt(variance + norm_epsilon) * extras[2] + extras[3]


LEVELS = 32767.0
CODES = 256.0
MESH = pl.DeviceIdType.MESH


def padded_rows(rows):
    return -(-(rows + 1) // 16) * 16


def lanes_of(count):
    return -(-count // 128) * 128


def diagonal(count, width):
    first = lax.broadcasted_iota(jnp.int32, (count, width), 0)
    second = lax.broadcasted_iota(jnp.int32, (count, width), 1)
    return first == second


def encode(value, rows):
    count, width = value.shape
    row_index = lax.broadcasted_iota(jnp.int32, (count, width), 0)
    value = jnp.where(row_index < rows, value, 0.0)
    top = jnp.maximum(jnp.max(jnp.abs(value), axis=1, keepdims=True), 1e-30)
    code = jnp.ceil(jnp.log2(top) * CODES + 0.01)
    scaled = value * (jnp.exp2(code * (-1.0 / CODES)) * LEVELS)
    near = jnp.where(diagonal(count, lanes_of(count)), code, 0.0)
    code_row = jnp.sum(near, axis=0, keepdims=True)
    if width > lanes_of(count):
        rest = jnp.zeros((1, width - lanes_of(count)), jnp.float32)
        code_row = jnp.concatenate([code_row, rest], axis=1)
    out = jnp.where(row_index == rows, jnp.broadcast_to(code_row, (count, width)), scaled)
    out = jnp.clip(jnp.round(out), -LEVELS, LEVELS)
    return out.astype(jnp.int32).astype(jnp.int16)


def decode(block, rows):
    count, width = block.shape
    value = block.astype(jnp.int32).astype(jnp.float32)
    code_row = value[rows : rows + 1, : lanes_of(count)]
    near = jnp.where(diagonal(count, lanes_of(count)), code_row, 0.0)
    code = jnp.sum(near, axis=1, keepdims=True)
    return value * (jnp.exp2(code * (1.0 / CODES)) * (1.0 / LEVELS))


def refresh_kernel(
    sizes, grad_ref, pixel_ref, student_ref, teacher_ref, moment1_ref, moment2_ref, fix_ref,
    gradient_ref, table_ref, other_ref,
    all_ref, pre_ref, out_ref, in_ref, space_ref, pair_sem, out_sem, in_sem, pix_sem, go_sem, come_sem,
):
    DP, F, C = sizes
    rows = student_ref.shape[0]
    d, f, c = lax.axis_index("dp"), lax.axis_index("fsdp"), lax.axis_index("crop")
    partner = lax.rem(c + 1, C)

    barrier = pltpu.get_barrier_semaphore()
    pl.semaphore_signal(barrier, inc=1, device_id={"crop": partner}, device_id_type=MESH)
    for r in range(1, DP):
        pl.semaphore_signal(barrier, inc=1, device_id={"dp": lax.rem(d + r, DP)}, device_id_type=MESH)
    for r in range(1, F):
        pl.semaphore_signal(barrier, inc=1, device_id={"fsdp": lax.rem(f + r, F)}, device_id_type=MESH)

    for b in range(DP):
        for k in range(C):
            j = b * C + k
            all_ref[k, b, 0:rows] = grad_ref[0, j * rows : (j + 1) * rows]
            all_ref[k, b, rows:] = jnp.zeros((all_ref.shape[2] - rows, all_ref.shape[3]), jnp.float32)
    pl.semaphore_wait(barrier, DP - 1 + 1 + F - 1)
    order = [DP - r for r in range(1, DP)] + [0]
    sends = []
    for r in order:
        at = lax.rem(d + r, DP)
        copy = pltpu.make_async_remote_copy(
            src_ref=all_ref.at[partner, at], dst_ref=pre_ref.at[lax.rem(d + r, DP)],
            send_sem=pair_sem.at[0, r], recv_sem=pair_sem.at[1, r],
            device_id={"crop": partner}, device_id_type=MESH,
        )
        copy.start()
        sends.append(copy)
    blocks = []
    total = None
    for number, r in enumerate(order):
        at = lax.rem(d + r, DP)
        sends[number].wait_recv()
        chip = all_ref[c, at] + pre_ref[at]
        if r == 0:
            total = chip
            break
        out_ref[r] = encode(chip, rows)
        copy = pltpu.make_async_remote_copy(
            src_ref=out_ref.at[r], dst_ref=in_ref.at[r],
            send_sem=out_sem.at[r], recv_sem=in_sem.at[r],
            device_id={"dp": at}, device_id_type=MESH,
        )
        copy.start()
        blocks.append(copy)
    pixel_copy = pltpu.make_async_remote_copy(
        src_ref=pixel_ref, dst_ref=other_ref, send_sem=pix_sem.at[0], recv_sem=pix_sem.at[1],
        device_id={"crop": lax.rem(c + 1, C)}, device_id_type=MESH,
    )
    pixel_copy.start()

    for number, copy in enumerate(blocks):
        copy.wait_recv()
        total = total + decode(in_ref[order[number]], rows)
    gradient = total[0:rows]
    gradient_ref[...] = gradient

    student = student_ref[...]
    first_moment = beta_one * moment1_ref[...] + (1.0 - beta_one) * gradient
    second_moment = beta_two * moment2_ref[...] + (1.0 - beta_two) * gradient * gradient
    update = (
        first_moment / fix_ref[0] / (jnp.sqrt(second_moment / fix_ref[1]) + adam_epsilon)
        + weight_decay * student
    )
    student_new = student - learn_rate * update
    space_ref[rows:] = jnp.zeros((space_ref.shape[0] - rows, space_ref.shape[1]), jnp.float32)
    space_ref[0:rows] = fix_ref[2] * teacher_ref[...] + (1.0 - fix_ref[2]) * student_new
    table_ref[f, d, c] = encode(space_ref[...], rows)

    def pass_on(at, to):
        number = len(sends) - DP
        copy = pltpu.make_async_remote_copy(
            src_ref=table_ref.at[at], dst_ref=table_ref.at[at],
            send_sem=go_sem.at[number], recv_sem=come_sem.at[at],
            device_id=to, device_id_type=MESH,
        )
        copy.start()
        sends.append(copy)

    def arrive(at):
        pltpu.make_async_copy(table_ref.at[at], table_ref.at[at], come_sem.at[at]).wait()

    row, column = d // 2, lax.rem(d, 2)
    beside = row * 2 + 1 - column
    across = (1 - row) * 2 + column
    corner = (1 - row) * 2 + 1 - column
    turn = 1 - 2 * (2 * f // F)

    def layer(q):
        return lax.rem(f + q * turn + F, F)

    def relay(q):
        for near, far in ((beside, across), (across, beside)):
            at = (layer(q), near, c)
            arrive(at)
            if (q % 2 == 0) == (near is beside):
                pass_on(at, {"dp": far})
            pass_on(at, {"crop": partner})

    for q in range(F):
        at = (layer(q), d, c)
        if q == 0:
            for r in range(1, F):
                pass_on(at, {"fsdp": layer(r)})
        else:
            arrive(at)
        pass_on(at, {"dp": beside})
        pass_on(at, {"dp": across})
        pass_on(at, {"crop": partner})
        if q == 0:
            relay(0)
        elif q > 1:
            relay(q - 1)
    if F > 1:
        relay(F - 1)
    for q in range(F):
        at = (layer(q), corner, c)
        arrive(at)
        pass_on(at, {"crop": partner})
    for q in range(F):
        for r in range(DP):
            arrive((layer(q), lax.rem(d + r, DP), partner))
    pixel_copy.wait()
    for copy in blocks + sends:
        copy.wait_send()


def tokens_kernel(
    sizes, table_ref, own_ref, other_ref, gradient_ref, student_ref, teacher_ref, moment1_ref, moment2_ref,
    pick_ref, fix_ref,
    student_out, moment1_out, moment2_out, teacher_out, update_out, tokens_ref,
    flat_ref, high_ref, low_ref, x_ref,
):
    DP, F, C = sizes
    student, gradient = student_ref[...], gradient_ref[...]
    first_moment = beta_one * moment1_ref[...] + (1.0 - beta_one) * gradient
    second_moment = beta_two * moment2_ref[...] + (1.0 - beta_two) * gradient * gradient
    update = (
        first_moment / fix_ref[0] / (jnp.sqrt(second_moment / fix_ref[1]) + adam_epsilon)
        + weight_decay * student
    )
    student_new = student - learn_rate * update
    student_out[...] = student_new
    moment1_out[...] = first_moment
    moment2_out[...] = second_moment
    teacher_out[...] = fix_ref[2] * teacher_ref[...] + (1.0 - fix_ref[2]) * student_new
    update_out[...] = update
    pix_size, patch_count = own_ref.shape
    columns = table_ref.shape[-1]
    width = flat_ref.shape[1]
    rows = flat_ref.shape[0] // (DP * C)
    base = pix_size + patch_count
    over = (((0,), (0,)), ((), ()))

    for i in range(F):
        for j in range(DP * C):
            block = decode(table_ref[i, j // C, j % C], rows)
            flat_ref[j * rows : (j + 1) * rows, i * columns : (i + 1) * columns] = block[0:rows]
    weight = flat_ref[0:pix_size]
    high = weight.astype(jnp.bfloat16)
    high_ref[...] = high
    low_ref[...] = (weight - high.astype(jnp.float32)).astype(jnp.bfloat16)
    flat_ref[pix_size:base] = flat_ref[pix_size:base] + flat_ref[base + 1 : base + 2]

    gain, shift = flat_ref[base + 2 : base + 3], flat_ref[base + 3 : base + 4]

    def normed(x):
        average = jnp.mean(x, axis=-1, keepdims=True)
        centered = x - average
        variance = jnp.mean(centered * centered, axis=-1, keepdims=True)
        return centered * lax.rsqrt(variance + norm_epsilon) * gain + shift

    class_row = normed(flat_ref[base : base + 1])
    for k in range(C):
        pixels = jnp.where(pick_ref[0, k] == lax.axis_index("crop"), own_ref[...], other_ref[...])
        for i in range(F):
            part = slice(i * columns, (i + 1) * columns)
            x_ref[:, part] = (
                lax.dot_general(pixels, high_ref[:, part], over, preferred_element_type=jnp.float32)
                + lax.dot_general(pixels, low_ref[:, part], over, preferred_element_type=jnp.float32)
                + flat_ref[pix_size:base, part]
            )
        tokens_ref[0:1, k] = class_row
        step = 32
        for start in range(0, patch_count, step):
            rows_now = normed(x_ref[start : start + step])
            tokens_ref[start + 1 : start + 1 + step, k] = rows_now


def kernels(grad_parts, student, teacher, moment1, moment2, step_count, pixels, assign, sizes):
    DP, F, C = sizes
    rows, columns = student.shape
    spare = padded_rows(rows)
    step_value = step_count[0].astype(jnp.float32)
    fixes = jnp.stack(
        [
            1.0 - jnp.power(jnp.float32(beta_one), step_value),
            1.0 - jnp.power(jnp.float32(beta_two), step_value),
            1.0 - (1.0 - momentum_base) * (jnp.cos(math.pi * step_value / plan_length) + 1.0) / 2.0,
        ]
    )
    own = pixels[0, 0].T
    here = pl.BlockSpec(memory_space=pltpu.VMEM)
    scalars = pl.BlockSpec(memory_space=pltpu.SMEM)
    count = DP * C
    gradient, table, other = pl.pallas_call(
        functools.partial(refresh_kernel, sizes),
        out_shape=(
            jax.ShapeDtypeStruct((rows, columns), jnp.float32),
            jax.ShapeDtypeStruct((F, DP, C, spare, columns), jnp.int16),
            jax.ShapeDtypeStruct(own.shape, own.dtype),
        ),
        in_specs=[here] * 6 + [scalars],
        out_specs=(here,) * 3,
        scratch_shapes=[
            pltpu.VMEM((C, DP, spare, columns), jnp.float32),
            pltpu.VMEM((DP, spare, columns), jnp.float32),
            pltpu.VMEM((DP, spare, columns), jnp.int16),
            pltpu.VMEM((DP, spare, columns), jnp.int16),
            pltpu.VMEM((spare, columns), jnp.float32),
            pltpu.SemaphoreType.DMA((2, DP)),
            pltpu.SemaphoreType.DMA((DP,)),
            pltpu.SemaphoreType.DMA((DP,)),
            pltpu.SemaphoreType.DMA((2,)),
            pltpu.SemaphoreType.DMA((F - 1 + F * 7,)),
            pltpu.SemaphoreType.DMA((F, DP, C)),
        ],
        compiler_params=pltpu.CompilerParams(collective_id=0, has_side_effects=True),
    )(grad_parts, own, student, teacher, moment1, moment2, fixes)
    pix_size, patch_count = own.shape
    width = columns * F
    *results, tokens = pl.pallas_call(
        functools.partial(tokens_kernel, sizes),
        out_shape=(jax.ShapeDtypeStruct((rows, columns), jnp.float32),) * 5
        + (jax.ShapeDtypeStruct((patch_count + 1, C, width), jnp.float32),),
        in_specs=[here] * 8 + [scalars] * 2,
        out_specs=(here,) * 6,
        scratch_shapes=[
            pltpu.VMEM((rows * count, width), jnp.float32),
            pltpu.VMEM((pix_size, width), jnp.bfloat16),
            pltpu.VMEM((pix_size, width), jnp.bfloat16),
            pltpu.VMEM((patch_count, width), jnp.float32),
        ],
    )(table, own, other, gradient, student, teacher, moment1, moment2, assign, fixes)
    return (*results, tokens.transpose(1, 0, 2)[None])


def shards(grad_parts, student, teacher, moment1, moment2, step_count, pixels, assign):
    gradient = lax.psum_scatter(grad_parts[0], ("dp", "crop"), scatter_dimension=0, tiled=True)
    student_new, first_moment, second_moment, teacher_new, update = optimize(
        gradient, student, teacher, moment1, moment2, step_count
    )
    column_block = lax.all_gather(teacher_new, "fsdp", axis=1, tiled=True)
    gathered = lax.all_gather(column_block, ("dp", "crop"), axis=0, tiled=True)
    own_tokens = embed(pixels[:, 0], gathered)
    both = lax.all_gather(own_tokens[:, None], "crop", axis=1, tiled=True)
    teacher_tokens = jnp.where((assign == 0)[:, :, None, None], both[:, 0:1], both[:, 1:2])
    return (student_new, first_moment, second_moment, teacher_new, update, teacher_tokens)


def solution(mesh):
    placed = (
        P(("dp", "crop"), None, "fsdp"),
        P(("dp", "crop"), "fsdp"),
        P(("dp", "crop"), "fsdp"),
        P(("dp", "crop"), "fsdp"),
        P(("dp", "crop"), "fsdp"),
        P(),
        P(("dp", "fsdp"), "crop", None, None),
        P(("dp", "fsdp"), None),
    )
    sizes = (mesh.shape["dp"], mesh.shape["fsdp"], mesh.shape["crop"])

    def run(*args):
        grad_parts, student, pixels = args[0], args[1], args[6]
        fits = (
            student.shape[1] % 128 == 0
            and padded_rows(student.shape[0]) <= student.shape[1]
            and pixels.shape[:2] == (1, 1)
            and grad_parts.shape[0] == 1
            and sizes[0] == 4
            and sizes[2] == 2
        )
        return kernels(*args, sizes) if fits else shards(*args)

    return jax.shard_map(
        run,
        mesh=mesh,
        in_specs=placed,
        out_specs=(
            P(("dp", "crop"), "fsdp"),
            P(("dp", "crop"), "fsdp"),
            P(("dp", "crop"), "fsdp"),
            P(("dp", "crop"), "fsdp"),
            P(("dp", "crop"), "fsdp"),
            P(("dp", "fsdp"), None, None, None),
        ),
        check_vma=False,
    )
```
